32 devices in a mesh: rep: 8 (over z, x), rows: 4 (over y, core).
Axes of the slice: x: 2, y: 2, z: 4, core: 2. Of those that a mesh axis runs over, the one named last changes fastest.
Arguments:
- pooled_grad: bfloat16 [32768, 2, 128], P(('rep', 'rows')), may hold values from -6 to 6
- slot_source: int32 [32, 4, 1024], P(('rep', 'rows')), may hold values from 0 to 2047, as said below
- slot_target: int32 [32, 4, 1024], P(('rep', 'rows')), may hold values from 0 to 8191, as said below
- slot_count: int32 [32, 4], P(('rep', 'rows')), may hold values from 128 to 1024, as said below
- table_rows: float32 [2, 16384, 128], P(None, 'rows'), may hold values from -1.5 to 1.5
- accum: float32 [2, 16384], P(None, 'rows'), may hold values from 0.01 to 1
Outputs:
- new_rows: float32 [2, 16384, 128], P(None, 'rows')
- new_accum: float32 [2, 16384], P(None, 'rows')
The draws below stay inside these ranges and needn't reach their ends.
Inputs may be any that keep to these rules, and one draw needn't show every extreme that they name: `slot_source`: entry q encodes a local sample q // 2 and a table q % 2; the table agrees with that of slot_target at the same slot. `slot_target`: entry t encodes a table t // 4096 and a row t % 4096 of the owner's shard; rows repeat across slots and senders. `slot_count`: slots at or past the count carry no lookup; every sender fills all slots to some owner.
All inputs are finite; a program needn't handle non-finite values.
Results may differ from the reference program's by a relative error of at most 0.0003.
Values may be sent and summed in bfloat16 or wider, within the bound.
A program may use at most 64 MiB of HBM per device.

```python
import math
import jax
import jax.numpy as jnp
from jax import lax

W = 128
ROWS_DEV = 4096
TABLES = 2
SAMP_DEV = 1024
OWNERS = 4
SENDERS = 32
ROWS = 16384
SAMPLES = 32768
CAP = 1024


def layout(key):
    folded = jax.random.fold_in(key, 4242)
    subkeys = jax.random.split(folded, 8)
    owner_ids = jnp.arange(OWNERS, dtype=jnp.int32)
    shape = (SENDERS, OWNERS, CAP)
    sample = jax.random.randint(subkeys[2], shape, 0, SAMP_DEV, dtype=jnp.int32)
    table_ids = jax.random.randint(subkeys[3], shape, 0, TABLES, dtype=jnp.int32)
    hot_count = ROWS_DEV // 16
    hot_rows = jax.random.randint(subkeys[4], (OWNERS, TABLES, hot_count), 0, ROWS_DEV, dtype=jnp.int32)
    pick_hot = jax.random.randint(subkeys[5], shape, 0, 4, dtype=jnp.int32) == 0
    hot_pick = jax.random.randint(subkeys[6], shape, 0, hot_count, dtype=jnp.int32)
    cold_rows = jax.random.randint(subkeys[7], shape, 0, ROWS_DEV, dtype=jnp.int32)
    owner_grid = jnp.broadcast_to(owner_ids[None, :, None], shape)
    chosen_hot = hot_rows[owner_grid, table_ids, hot_pick]
    row_ids = jnp.where(pick_hot, chosen_hot, cold_rows).astype(jnp.int32)
    source = (sample * TABLES + table_ids).astype(jnp.int32)
    target = (table_ids * ROWS_DEV + row_ids).astype(jnp.int32)
    return (source, target)


def draw_slot_source(key, part):
    return layout(key)[0]


def draw_slot_target(key, part):
    return layout(key)[1]


def draw_slot_count(key, part):
    folded = jax.random.fold_in(key, 9191)
    first_key, second_key = jax.random.split(folded, 2)
    owner_ids = jnp.arange(OWNERS, dtype=jnp.int32)
    busy_owner = jax.random.randint(first_key, (SENDERS,), 0, OWNERS, dtype=jnp.int32)
    spread = jax.random.randint(second_key, (SENDERS, OWNERS), CAP // 8, CAP + 1, dtype=jnp.int32)
    is_busy = owner_ids[None, :] == busy_owner[:, None]
    return jnp.where(is_busy, CAP, spread).astype(jnp.int32)


def block_scale(key, dims, shards, smallest, high):
    def one(axis_at, blocks):
        heights = jax.random.uniform(jax.random.fold_in(jax.random.fold_in(key, 6), axis_at), (blocks,), jnp.float32, smallest / len(shards), high / len(shards))
        return jnp.repeat(jnp.exp(heights), dims[axis_at] // blocks).reshape((-1,) + (1,) * (len(dims) - axis_at - 1))

    gain = one(*shards[0])
    for cut in shards[1:]:
        gain = gain * one(*cut)
    return gain


def centred(key, dims, scale, limit, pieces=(), kind=jnp.bfloat16):
    gain = block_scale(key, dims, pieces, -0.22, 0.18) if pieces else 1.0
    result = jax.random.normal(key, dims, jnp.float32) * scale * gain
    return jnp.minimum(jnp.maximum(result, -limit), limit).astype(kind)


def setup_inputs(seed: int = 0) -> dict:
    arg_keys = jax.random.split(jax.random.key(seed), 7)
    pooled_grad = centred(arg_keys[0], (SAMPLES, TABLES, W), 1.0, 6.0, ((0, 32),))
    slot_source = draw_slot_source(jax.random.fold_in(arg_keys[6], 71), 0)
    slot_target = draw_slot_target(jax.random.fold_in(arg_keys[6], 71), 0)
    slot_count = draw_slot_count(jax.random.fold_in(arg_keys[6], 71), 0)
    table_rows = centred(arg_keys[4], (TABLES, ROWS, W), 0.1, 1.5, ((1, 4),), jnp.float32)
    accum = jnp.clip(jnp.exp(math.log(1.0) - 4.6051702 * jax.random.uniform(arg_keys[5], (TABLES, ROWS), jnp.float32) ** block_scale(arg_keys[5], (TABLES, ROWS), ((1, 4),), -0.2, 0.2)), 0.01, 1.0)
    return {"pooled_grad": pooled_grad, "slot_source": slot_source, "slot_target": slot_target, "slot_count": slot_count, "table_rows": table_rows, "accum": accum}


LEARN_RATE = 0.1
EPSILON = 1e-06

def reference(pooled_grad, slot_source, slot_target, slot_count, table_rows, accum):
    flat_grad = pooled_grad.reshape(SENDERS * SAMP_DEV * TABLES, W)
    slot_ids = jnp.arange(CAP, dtype=jnp.int32)
    owner_ids = jnp.arange(OWNERS, dtype=jnp.int32)

    def add_sender(summed, inputs):
        sender, source, target, counts = inputs
        filled = slot_ids[None, :] < counts[:, None]
        picked = flat_grad[sender * (SAMP_DEV * TABLES) + source].astype(jnp.float32)
        picked = jnp.where(filled[:, :, None], picked, jnp.zeros_like(picked))
        table_ids = target // ROWS_DEV
        row_ids = target % ROWS_DEV
        segment = table_ids * ROWS + owner_ids[:, None] * ROWS_DEV + row_ids
        summed = summed.at[segment.reshape(-1)].add(picked.reshape(-1, W))
        return (summed, None)
    start = jnp.zeros((TABLES * ROWS, W), jnp.float32)
    senders = jnp.arange(SENDERS, dtype=jnp.int32)
    summed, _ = lax.scan(add_sender, start, (senders, slot_source, slot_target, slot_count))
    row_grad = summed.reshape(TABLES, ROWS, W)
    new_accum = accum + lax.optimization_barrier(jnp.mean(row_grad * row_grad, axis=2))
    new_rows = table_rows - LEARN_RATE * row_grad / (jnp.sqrt(new_accum)[:, :, None] + EPSILON)
    return (new_rows, new_accum)
```

```python
import functools

import jax
import jax.numpy as jnp
from jax import lax
from jax.experimental import pallas as pl
from jax.experimental.pallas import tpu as pltpu
from jax.sharding import PartitionSpec as P

LEARN_RATE = 0.1
EPSILON = 1e-06
CODE_MAX = 32000.0
TINY = 1e-30
UNROLL = 8
BLOCK = 512


def scatter_kernel(order_ref, source_ref, target_ref, *refs):
    senders = source_ref.shape[0]
    grad_refs, out_ref = refs[:senders], refs[senders]
    wide_refs, sum_refs = refs[senders + 1 : 2 * senders + 1], refs[2 * senders + 1 :]
    rows = out_ref.shape[0]
    slots = source_ref.shape[1]
    for wide_ref, grad_ref in zip(wide_refs, grad_refs):
        wide_ref[...] = grad_ref[...].astype(jnp.float32)
    zeros = jnp.zeros((BLOCK, out_ref.shape[1]), jnp.float32)

    @pl.loop(0, rows // BLOCK)
    def _(block):
        for sum_ref in sum_refs:
            sum_ref[pl.ds(pl.multiple_of(block * BLOCK, BLOCK), BLOCK), :] = zeros

    owners = [order_ref[place] for place in range(senders)]

    @pl.loop(0, slots // UNROLL)
    def _(step):
        for sub in range(UNROLL):
            slot = step * UNROLL + sub
            for place in range(senders):
                row = target_ref[owners[place], slot]
                picked = wide_refs[place][pl.ds(source_ref[owners[place], slot], 1), :]
                sum_refs[place][pl.ds(row, 1), :] += picked

    @pl.loop(0, rows // BLOCK)
    def _(block):
        at = pl.ds(pl.multiple_of(block * BLOCK, BLOCK), BLOCK)
        total = sum_refs[0][at, :]
        for sum_ref in sum_refs[1:]:
            total += sum_ref[at, :]
        out_ref[at, :] = total


def scatter(order, sources, targets, grads, rows):
    senders, slots = sources.shape
    feature = grads[0].shape[1]
    samples = grads[0].shape[0]
    smem = pl.BlockSpec(memory_space=pltpu.SMEM)
    vmem = pl.BlockSpec(memory_space=pltpu.VMEM)
    return pl.pallas_call(
        scatter_kernel,
        out_shape=jax.ShapeDtypeStruct((rows, feature), jnp.float32),
        in_specs=[smem] * 3 + [vmem] * senders,
        out_specs=vmem,
        scratch_shapes=[pltpu.VMEM((samples, feature), jnp.float32)] * senders
        + [pltpu.VMEM((rows + 8, feature), jnp.float32)] * senders,
        compiler_params=pltpu.CompilerParams(vmem_limit_bytes=48 << 20),
    )(order, sources, targets, *grads)


def encode(values):
    largest = jnp.max(jnp.abs(values), axis=-1)
    scale = jnp.maximum(largest, TINY) / CODE_MAX
    return jnp.round(values / scale[..., None]).astype(jnp.int16), scale


def decode(codes, scale):
    return codes.astype(jnp.float32) * scale[..., None]


def shards(pooled_grad, slot_source, slot_target, slot_count, table_rows, accum):
    tables, feature = pooled_grad.shape[1:]
    rows_dev = table_rows.shape[1]
    rows = tables * rows_dev
    owner_total, slot_total = slot_source.shape[1:]
    copies = lax.axis_size("rep")
    me = lax.axis_index("rows")
    grads = pooled_grad.reshape(-1, feature)
    slot_ids = jnp.arange(slot_total, dtype=jnp.int32)
    filled = slot_ids[None, :] < slot_count[0][:, None]
    targets = jnp.where(filled, slot_target[0], rows)
    lookups = lax.all_to_all(
        jnp.stack([slot_source[0], targets], axis=1), "rows", split_axis=0, concat_axis=0, tiled=True
    )
    pieces = {0: grads}
    span = owner_total // 2
    while span:
        swap = [(one, one ^ span) for one in range(owner_total)]
        for place, piece in list(pieces.items()):
            pieces[place ^ span] = lax.ppermute(piece, "rows", swap)
        span //= 2
    order = me ^ jnp.arange(owner_total, dtype=jnp.int32)
    partial_grad = scatter(
        order, lookups[:, 0], lookups[:, 1], [pieces[place] for place in range(owner_total)], rows
    )
    share = rows // copies
    codes, scale = encode(partial_grad.reshape(copies, share, feature))
    got_codes = lax.all_to_all(codes, "rep", split_axis=0, concat_axis=0, tiled=True)
    got_scale = lax.all_to_all(scale, "rep", split_axis=0, concat_axis=0, tiled=True)
    row_grad = jnp.sum(decode(got_codes, got_scale), axis=0)
    state = lax.dynamic_slice(accum.reshape(-1), (lax.axis_index("rep") * share,), (share,))
    updated = state + jnp.mean(row_grad * row_grad, axis=1)
    move_codes, move_scale = encode(row_grad / (jnp.sqrt(updated)[:, None] + EPSILON))
    all_codes = lax.all_gather(move_codes, "rep", tiled=True)
    all_side = lax.all_gather(jnp.stack([updated, move_scale]), "rep")
    new_accum = all_side[:, 0].reshape(tables, rows_dev)
    all_scale = all_side[:, 1].reshape(tables, rows_dev)
    move = decode(all_codes.reshape(tables, rows_dev, feature), all_scale)
    return table_rows - LEARN_RATE * move, new_accum


def solution(mesh):
    in_specs = (
        P(("rep", "rows"), None, None),
        P(("rep", "rows"), None, None),
        P(("rep", "rows"), None, None),
        P(("rep", "rows"), None),
        P(None, "rows", None),
        P(None, "rows"),
    )
    out_specs = (P(None, "rows", None), P(None, "rows"))
    return jax.shard_map(shards, mesh=mesh, in_specs=in_specs, out_specs=out_specs, check_vma=False)
```

```python
import functools

import jax
import jax.numpy as jnp
from jax import lax
from jax.experimental import pallas as pl
from jax.experimental.pallas import tpu as pltpu
from jax.sharding import PartitionSpec as P

LEARN_RATE = 0.1
EPSILON = 1e-06
CODE_MAX = 32000.0
TINY = 1e-30
UNROLL = 8
BLOCK = 512
LANES = 128


def scatter_kernel(order_ref, source_ref, target_ref, *refs):
    senders = source_ref.shape[0]
    grad_refs, (out_ref, scale_ref) = refs[:senders], refs[senders : senders + 2]
    wide_refs, sum_refs = refs[senders + 2 : 2 * senders + 2], refs[2 * senders + 2 :]
    rows = out_ref.shape[0]
    slots = source_ref.shape[1]
    for wide_ref, grad_ref in zip(wide_refs, grad_refs):
        wide_ref[...] = grad_ref[...].astype(jnp.float32)
    zeros = jnp.zeros((BLOCK, out_ref.shape[1]), jnp.float32)

    @pl.loop(0, rows // BLOCK)
    def _(block):
        for sum_ref in sum_refs:
            sum_ref[pl.ds(pl.multiple_of(block * BLOCK, BLOCK), BLOCK), :] = zeros

    owners = [order_ref[place] for place in range(senders)]

    @pl.loop(0, slots // UNROLL)
    def _(step):
        for sub in range(UNROLL):
            slot = step * UNROLL + sub
            for place in range(senders):
                row = target_ref[owners[place], slot]
                picked = wide_refs[place][pl.ds(source_ref[owners[place], slot], 1), :]
                sum_refs[place][pl.ds(row, 1), :] += picked

    eye = diagonal()

    @pl.loop(0, rows // LANES)
    def _(block):
        at = pl.ds(pl.multiple_of(block * LANES, LANES), LANES)
        total = sum_refs[0][at, :]
        for sum_ref in sum_refs[1:]:
            total += sum_ref[at, :]
        codes, scale = encode(total)
        out_ref[at, :] = codes
        scale_ref[block] = to_row(eye, scale)


def scatter(order, sources, targets, grads, rows):
    senders, slots = sources.shape
    feature = grads[0].shape[1]
    samples = grads[0].shape[0]
    smem = pl.BlockSpec(memory_space=pltpu.SMEM)
    vmem = pl.BlockSpec(memory_space=pltpu.VMEM)
    return pl.pallas_call(
        scatter_kernel,
        out_shape=(
            jax.ShapeDtypeStruct((rows, feature), jnp.int16),
            jax.ShapeDtypeStruct((rows // LANES, 1, LANES), jnp.float32),
        ),
        in_specs=[smem] * 3 + [vmem] * senders,
        out_specs=(vmem, vmem),
        scratch_shapes=[pltpu.VMEM((samples, feature), jnp.float32)] * senders
        + [pltpu.VMEM((rows + 8, feature), jnp.float32)] * senders,
        compiler_params=pltpu.CompilerParams(vmem_limit_bytes=48 << 20),
    )(order, sources, targets, *grads)


def diagonal():
    shape = (LANES, LANES)
    return lax.broadcasted_iota(jnp.int32, shape, 0) == lax.broadcasted_iota(jnp.int32, shape, 1)


def to_row(eye, column):
    return jnp.sum(jnp.where(eye, column, 0.0), axis=0, keepdims=True)


def to_column(eye, row):
    return jnp.sum(jnp.where(eye, row, 0.0), axis=1, keepdims=True)


def encode(values):
    largest = jnp.max(jnp.abs(values), axis=1, keepdims=True)
    scale = jnp.maximum(largest, TINY) * (1.0 / CODE_MAX)
    return jnp.round(values * (1.0 / scale)).astype(jnp.int32).astype(jnp.int16), scale


def decode(codes, scale):
    return codes.astype(jnp.int32).astype(jnp.float32) * scale


def reduce_kernel(code_ref, scale_ref, state_ref, out_ref, side_ref, *scratch):
    near_code, near_scale, sum_code, sum_scale, far_code, far_scale, send_sem, recv_sem = scratch
    copies, share, _ = code_ref.shape
    blocks = share // LANES
    pairs = copies // 2
    me = lax.axis_index("rep")
    pair, side = me // 2, lax.rem(me, 2)
    partner = pair * 2 + (1 - side)
    eye = diagonal()

    def other(step):
        return lax.rem(pair + step, pairs)

    def back(step):
        return lax.rem(pair + pairs - step, pairs)

    def send(phase, kind, step, source, target, device):
        copy = pltpu.make_async_remote_copy(
            src_ref=source,
            dst_ref=target,
            send_sem=send_sem.at[phase, kind, step],
            recv_sem=recv_sem.at[phase, kind, step],
            device_id={"rep": device},
            device_id_type=pl.DeviceIdType.MESH,
        )
        copy.start()
        return copy

    barrier = pltpu.get_barrier_semaphore()
    for peer in [partner] + [other(step) * 2 + side for step in range(1, pairs)]:
        pl.semaphore_signal(barrier, inc=1, device_id={"rep": peer}, device_id_type=pl.DeviceIdType.MESH)
    pl.semaphore_wait(barrier, pairs)

    steps = list(range(1, pairs)) + [0]
    near, far, hand, last = {}, {}, {}, {}
    for step in steps:
        chunk = other(step) * 2 + (1 - side)
        near[step] = (
            send(0, 0, step, code_ref.at[chunk], near_code.at[step], partner),
            send(0, 1, step, scale_ref.at[chunk], near_scale.at[step], partner),
        )
    for step in steps[:-1]:
        for copy in near[step]:
            copy.wait_recv()
        chunk = other(step) * 2 + side

        @pl.loop(0, blocks)
        def _(block):
            at = pl.ds(pl.multiple_of(block * LANES, LANES), LANES)
            total = decode(code_ref[chunk, at, :], to_column(eye, scale_ref[chunk, block]))
            total += decode(near_code[step, at, :], to_column(eye, near_scale[step, block]))
            codes, scale = encode(total)
            sum_code[step, at, :] = codes
            sum_scale[step, block] = to_row(eye, scale)

        far[step] = (
            send(1, 0, step, sum_code.at[step], far_code.at[step], chunk),
            send(1, 1, step, sum_scale.at[step], far_scale.at[step], chunk),
        )
    for copy in near[0]:
        copy.wait_recv()
    for step in steps[:-1]:
        for copy in far[step]:
            copy.wait_recv()

    @pl.loop(0, blocks)
    def _(block):
        at = pl.ds(pl.multiple_of(block * LANES, LANES), LANES)
        total = decode(code_ref[me, at, :], to_column(eye, scale_ref[me, block]))
        total += decode(near_code[0, at, :], to_column(eye, near_scale[0, block]))
        for step in steps[:-1]:
            total += decode(far_code[step, at, :], to_column(eye, far_scale[step, block]))
        codes, scale = encode(total)
        out_ref[me, at, :] = codes
        square = jnp.sum(total * total, axis=1, keepdims=True) * (1.0 / total.shape[1])
        updated = state_ref[me, block] + to_row(eye, square)
        side_ref[me, block, 0:1, :] = updated
        side_ref[me, block, 1:2, :] = to_row(eye, scale) / (jnp.sqrt(updated) + EPSILON)

    def share_out(phase, step, chunk, device):
        return (
            send(phase, 0, step, out_ref.at[chunk], out_ref.at[chunk], device),
            send(phase, 1, step, side_ref.at[chunk], side_ref.at[chunk], device),
        )

    for step in range(1, pairs):
        hand[step] = share_out(2, step, me, other(step) * 2 + side)
    last[0] = share_out(3, 0, me, partner)
    for step in range(1, pairs):
        for copy in hand[step]:
            copy.wait_recv()
        last[step] = share_out(3, step, back(step) * 2 + side, partner)
    for step in range(pairs):
        for copy in last[step]:
            copy.wait_recv()
    for group in (near, far, hand, last):
        for copies_of in group.values():
            for copy in copies_of:
                copy.wait_send()


def reduce_rep(codes, scales, state):
    copies, share, feature = codes.shape
    blocks = share // LANES
    pairs = copies // 2
    vmem = pl.BlockSpec(memory_space=pltpu.VMEM)
    code_room = pltpu.VMEM((pairs, share, feature), jnp.int16)
    scale_room = pltpu.VMEM((pairs, blocks, 1, LANES), jnp.float32)
    return pl.pallas_call(
        reduce_kernel,
        out_shape=(
            jax.ShapeDtypeStruct(codes.shape, jnp.int16),
            jax.ShapeDtypeStruct((copies, blocks, 2, LANES), jnp.float32),
        ),
        in_specs=[vmem] * 3,
        out_specs=(vmem, vmem),
        scratch_shapes=[code_room, scale_room] * 3
        + [pltpu.SemaphoreType.DMA((4, 2, pairs)), pltpu.SemaphoreType.DMA((4, 2, pairs))],
        compiler_params=pltpu.CompilerParams(
            collective_id=1, has_side_effects=True, vmem_limit_bytes=32 << 20
        ),
    )(codes, scales, state)


def shards(pooled_grad, slot_source, slot_target, slot_count, table_rows, accum):
    tables, feature = pooled_grad.shape[1:]
    rows_dev = table_rows.shape[1]
    rows = tables * rows_dev
    owner_total, slot_total = slot_source.shape[1:]
    copies = lax.axis_size("rep")
    me = lax.axis_index("rows")
    grads = pooled_grad.reshape(-1, feature)
    slot_ids = jnp.arange(slot_total, dtype=jnp.int32)
    filled = slot_ids[None, :] < slot_count[0][:, None]
    targets = jnp.where(filled, slot_target[0], rows)
    lookups = lax.all_to_all(
        jnp.stack([slot_source[0], targets], axis=1), "rows", split_axis=0, concat_axis=0, tiled=True
    )
    pieces = {0: grads}
    span = owner_total // 2
    while span:
        swap = [(one, one ^ span) for one in range(owner_total)]
        for place, piece in list(pieces.items()):
            pieces[place ^ span] = lax.ppermute(piece, "rows", swap)
        span //= 2
    order = me ^ jnp.arange(owner_total, dtype=jnp.int32)
    codes, scales = scatter(
        order, lookups[:, 0], lookups[:, 1], [pieces[place] for place in range(owner_total)], rows
    )
    share = rows // copies
    blocked = (copies, share // LANES, 1, LANES)
    all_codes, all_side = reduce_rep(
        codes.reshape(copies, share, feature), scales.reshape(blocked), accum.reshape(blocked)
    )
    new_accum = all_side[:, :, 0].reshape(tables, rows_dev)
    step = all_side[:, :, 1].reshape(tables, rows_dev, 1)
    move = all_codes.reshape(tables, rows_dev, feature).astype(jnp.float32) * step
    return table_rows - LEARN_RATE * move, new_accum


def solution(mesh):
    in_specs = (
        P(("rep", "rows"), None, None),
        P(("rep", "rows"), None, None),
        P(("rep", "rows"), None, None),
        P(("rep", "rows"), None),
        P(None, "rows", None),
        P(None, "rows"),
    )
    out_specs = (P(None, "rows", None), P(None, "rows"))
    return jax.shard_map(shards, mesh=mesh, in_specs=in_specs, out_specs=out_specs, check_vma=False)
```

```python
import functools
import math

import jax
import jax.numpy as jnp
from jax import lax
from jax.experimental import pallas as pl
from jax.experimental.pallas import tpu as pltpu
from jax.sharding import PartitionSpec as P

LEARN_RATE = 0.1
EPSILON = 1e-06
CODE_MAX = 32000.0
TINY = 1e-30
UNROLL = 8
BLOCK = 512
PARTS = 4
LANES = 128


def scatter_kernel(order_ref, source_ref, target_ref, *refs):
    senders = source_ref.shape[0]
    grad_refs, (out_ref, scale_ref) = refs[:senders], refs[senders : senders + 2]
    wide_refs, sum_refs = refs[senders + 2 : 2 * senders + 2], refs[2 * senders + 2 :]
    rows = out_ref.shape[0]
    slots = source_ref.shape[1]
    for wide_ref, grad_ref in zip(wide_refs, grad_refs):
        wide_ref[...] = grad_ref[...].astype(jnp.float32)
    zeros = jnp.zeros((BLOCK, out_ref.shape[1]), jnp.float32)

    @pl.loop(0, rows // BLOCK)
    def _(block):
        for sum_ref in sum_refs:
            sum_ref[pl.ds(pl.multiple_of(block * BLOCK, BLOCK), BLOCK), :] = zeros

    owners = [order_ref[place] for place in range(senders)]

    @pl.loop(0, slots // UNROLL)
    def _(step):
        for sub in range(UNROLL):
            slot = step * UNROLL + sub
            for place in range(senders):
                row = target_ref[owners[place], slot]
                picked = wide_refs[place][pl.ds(source_ref[owners[place], slot], 1), :]
                sum_refs[place][pl.ds(row, 1), :] += picked

    eye = diagonal()

    @pl.loop(0, rows // LANES)
    def _(block):
        at = pl.ds(pl.multiple_of(block * LANES, LANES), LANES)
        total = sum_refs[0][at, :]
        for sum_ref in sum_refs[1:]:
            total += sum_ref[at, :]
        codes, scale = encode(total)
        out_ref[at, :] = codes
        scale_ref[block] = to_row(eye, scale)


def scatter(order, sources, targets, grads, rows):
    senders, slots = sources.shape
    feature = grads[0].shape[1]
    samples = grads[0].shape[0]
    smem = pl.BlockSpec(memory_space=pltpu.SMEM)
    vmem = pl.BlockSpec(memory_space=pltpu.VMEM)
    return pl.pallas_call(
        scatter_kernel,
        out_shape=(
            jax.ShapeDtypeStruct((rows, feature), jnp.int16),
            jax.ShapeDtypeStruct((rows // LANES, 1, LANES), jnp.float32),
        ),
        in_specs=[smem] * 3 + [vmem] * senders,
        out_specs=(vmem, vmem),
        scratch_shapes=[pltpu.VMEM((samples, feature), jnp.float32)] * senders
        + [pltpu.VMEM((rows + 8, feature), jnp.float32)] * senders,
        compiler_params=pltpu.CompilerParams(vmem_limit_bytes=48 << 20),
    )(order, sources, targets, *grads)


def diagonal():
    shape = (LANES, LANES)
    return lax.broadcasted_iota(jnp.int32, shape, 0) == lax.broadcasted_iota(jnp.int32, shape, 1)


def to_row(eye, column):
    return jnp.sum(jnp.where(eye, column, 0.0), axis=0, keepdims=True)


def to_column(eye, row):
    return jnp.sum(jnp.where(eye, row, 0.0), axis=1, keepdims=True)


def encode(values):
    largest = jnp.max(jnp.abs(values), axis=1, keepdims=True)
    scale = jnp.maximum(largest, TINY) * (1.0 / CODE_MAX)
    return jnp.round(values * (1.0 / scale)).astype(jnp.int32).astype(jnp.int16), scale


def decode(codes, scale):
    return codes.astype(jnp.int32).astype(jnp.float32) * scale


def reduce_kernel(parts, code_ref, scale_ref, state_ref, out_ref, side_ref, *scratch):
    near_code, near_scale, sum_code, sum_scale, far_code, far_scale, send_sem, recv_sem = scratch
    copies, share, _ = code_ref.shape
    blocks = share // LANES
    pairs = copies // 2
    me = lax.axis_index("rep")
    pair, side = me // 2, lax.rem(me, 2)
    partner = pair * 2 + (1 - side)
    eye = diagonal()

    def other(step):
        return lax.rem(pair + step, pairs)

    def back(step):
        return lax.rem(pair + pairs - step, pairs)

    def send(phase, kind, step, part, source, target, device):
        copy = pltpu.make_async_remote_copy(
            src_ref=source,
            dst_ref=target,
            send_sem=send_sem.at[phase, kind, step, part],
            recv_sem=recv_sem.at[phase, kind, step, part],
            device_id={"rep": device},
            device_id_type=pl.DeviceIdType.MESH,
        )
        copy.start()
        return copy

    barrier = pltpu.get_barrier_semaphore()
    for peer in [partner] + [other(step) * 2 + side for step in range(1, pairs)]:
        pl.semaphore_signal(barrier, inc=1, device_id={"rep": peer}, device_id_type=pl.DeviceIdType.MESH)
    pl.semaphore_wait(barrier, pairs)

    steps = list(range(1, pairs)) + [0]
    part_blocks = blocks // parts
    near, far, hand, last = {}, {}, {}, {}

    def cut(ref, index, part):
        return ref.at[index, pl.ds(part * part_blocks, part_blocks)]

    def rows_of(ref, index, part):
        return ref.at[index, pl.ds(part * part_blocks * LANES, part_blocks * LANES)]

    def pair_sums(part):
        for step in steps[:-1]:
            for copy in near[step, part]:
                copy.wait_recv()
            chunk = other(step) * 2 + side

            @pl.loop(part * part_blocks, (part + 1) * part_blocks)
            def _(block):
                at = pl.ds(pl.multiple_of(block * LANES, LANES), LANES)
                total = decode(code_ref[chunk, at, :], to_column(eye, scale_ref[chunk, block]))
                total += decode(near_code[step, at, :], to_column(eye, near_scale[step, block]))
                codes, scale = encode(total)
                sum_code[step, at, :] = codes
                sum_scale[step, block] = to_row(eye, scale)

            far[step, part] = (
                send(1, 0, step, part, rows_of(sum_code, step, part), rows_of(far_code, step, part), chunk),
                send(1, 1, step, part, cut(sum_scale, step, part), cut(far_scale, step, part), chunk),
            )

    def share_out(phase, step, part, chunk, device):
        rows, rest = rows_of(out_ref, chunk, part), cut(side_ref, chunk, part)
        return send(phase, 0, step, part, rows, rows, device), send(phase, 1, step, part, rest, rest, device)

    def finish(part):
        for copy in near[0, part]:
            copy.wait_recv()
        for step in steps[:-1]:
            for copy in far[step, part]:
                copy.wait_recv()

        @pl.loop(part * part_blocks, (part + 1) * part_blocks)
        def _(block):
            at = pl.ds(pl.multiple_of(block * LANES, LANES), LANES)
            total = decode(code_ref[me, at, :], to_column(eye, scale_ref[me, block]))
            total += decode(near_code[0, at, :], to_column(eye, near_scale[0, block]))
            for step in steps[:-1]:
                total += decode(far_code[step, at, :], to_column(eye, far_scale[step, block]))
            codes, scale = encode(total)
            out_ref[me, at, :] = codes
            square = jnp.sum(total * total, axis=1, keepdims=True) * (1.0 / total.shape[1])
            updated = state_ref[me, block] + to_row(eye, square)
            side_ref[me, block, 0:1, :] = updated
            side_ref[me, block, 1:2, :] = to_row(eye, scale) / (jnp.sqrt(updated) + EPSILON)

        for step in range(1, pairs):
            hand[step, part] = share_out(2, step, part, me, other(step) * 2 + side)
        last[0, part] = share_out(3, 0, part, me, partner)

    def pass_on(part):
        for step in range(1, pairs):
            for copy in hand[step, part]:
                copy.wait_recv()
            last[step, part] = share_out(3, step, part, back(step) * 2 + side, partner)

    for part in range(parts):
        for step in steps:
            chunk = other(step) * 2 + (1 - side)
            near[step, part] = (
                send(0, 0, step, part, rows_of(code_ref, chunk, part), rows_of(near_code, step, part), partner),
                send(0, 1, step, part, cut(scale_ref, chunk, part), cut(near_scale, step, part), partner),
            )
    for turn in range(parts + 2):
        if turn < parts:
            pair_sums(turn)
        if 0 <= turn - 1 < parts:
            finish(turn - 1)
        if 0 <= turn - 2:
            pass_on(turn - 2)
    for key in last:
        for copy in last[key]:
            copy.wait_recv()
    for group in (near, far, hand, last):
        for sent in group.values():
            for copy in sent:
                copy.wait_send()


def reduce_rep(codes, scales, state):
    copies, share, feature = codes.shape
    blocks = share // LANES
    pairs = copies // 2
    vmem = pl.BlockSpec(memory_space=pltpu.VMEM)
    code_room = pltpu.VMEM((pairs, share, feature), jnp.int16)
    scale_room = pltpu.VMEM((pairs, blocks, 1, LANES), jnp.float32)
    parts = math.gcd(blocks, PARTS)
    semaphores = pltpu.SemaphoreType.DMA((4, 2, pairs, parts))
    return pl.pallas_call(
        functools.partial(reduce_kernel, parts),
        out_shape=(
            jax.ShapeDtypeStruct(codes.shape, jnp.int16),
            jax.ShapeDtypeStruct((copies, blocks, 2, LANES), jnp.float32),
        ),
        in_specs=[vmem] * 3,
        out_specs=(vmem, vmem),
        scratch_shapes=[code_room, scale_room] * 3
        + [semaphores, semaphores],
        compiler_params=pltpu.CompilerParams(
            collective_id=1, has_side_effects=True, vmem_limit_bytes=32 << 20
        ),
    )(codes, scales, state)


def shards(pooled_grad, slot_source, slot_target, slot_count, table_rows, accum):
    tables, feature = pooled_grad.shape[1:]
    rows_dev = table_rows.shape[1]
    rows = tables * rows_dev
    owner_total, slot_total = slot_source.shape[1:]
    copies = lax.axis_size("rep")
    me = lax.axis_index("rows")
    grads = pooled_grad.reshape(-1, feature)
    slot_ids = jnp.arange(slot_total, dtype=jnp.int32)
    filled = slot_ids[None, :] < slot_count[0][:, None]
    targets = jnp.where(filled, slot_target[0], rows)
    lookups = lax.all_to_all(
        jnp.stack([slot_source[0], targets], axis=1), "rows", split_axis=0, concat_axis=0, tiled=True
    )
    pieces = {0: grads}
    span = owner_total // 2
    while span:
        swap = [(one, one ^ span) for one in range(owner_total)]
        for place, piece in list(pieces.items()):
            pieces[place ^ span] = lax.ppermute(piece, "rows", swap)
        span //= 2
    order = me ^ jnp.arange(owner_total, dtype=jnp.int32)
    codes, scales = scatter(
        order, lookups[:, 0], lookups[:, 1], [pieces[place] for place in range(owner_total)], rows
    )
    share = rows // copies
    blocked = (copies, share // LANES, 1, LANES)
    all_codes, all_side = reduce_rep(
        codes.reshape(copies, share, feature), scales.reshape(blocked), accum.reshape(blocked)
    )
    new_accum = all_side[:, :, 0].reshape(tables, rows_dev)
    step = all_side[:, :, 1].reshape(tables, rows_dev, 1)
    move = all_codes.reshape(tables, rows_dev, feature).astype(jnp.float32) * step
    return table_rows - LEARN_RATE * move, new_accum


def solution(mesh):
    in_specs = (
        P(("rep", "rows"), None, None),
        P(("rep", "rows"), None, None),
        P(("rep", "rows"), None, None),
        P(("rep", "rows"), None),
        P(None, "rows", None),
        P(None, "rows"),
    )
    out_specs = (P(None, "rows", None), P(None, "rows"))
    return jax.shard_map(shards, mesh=mesh, in_specs=in_specs, out_specs=out_specs, check_vma=False)
```

```python
import functools
import math

import jax
import jax.numpy as jnp
from jax import lax
from jax.experimental import pallas as pl
from jax.experimental.pallas import tpu as pltpu
from jax.sharding import PartitionSpec as P

LEARN_RATE = 0.1
EPSILON = 1e-06
CODE_MAX = 32000.0
TINY = 1e-30
UNROLL = 16
BLOCK = 512
PARTS = 4
COST_BYTES = 20_000_000
LANES = 128


def scatter_kernel(places, slots, coded, order_ref, lookup_ref, *refs):
    count = len(places)
    grad_refs, refs = refs[:count], refs[count:]
    if coded:
        base_ref, out_ref, scale_ref, *refs = refs
    else:
        out_ref, *refs = refs
    wide_refs, sum_refs = refs[:count], refs[count:]
    rows, feature = out_ref.shape
    for wide_ref, grad_ref in zip(wide_refs, grad_refs):
        wide_ref[...] = grad_ref[...].astype(jnp.float32)
    zeros = jnp.zeros((BLOCK, feature), jnp.float32)

    @pl.loop(0, rows // BLOCK)
    def _(block):
        for sum_ref in sum_refs:
            sum_ref[pl.ds(pl.multiple_of(block * BLOCK, BLOCK), BLOCK), :] = zeros

    starts = [order_ref[place] * (2 * slots) for place in places]

    @pl.loop(0, slots // UNROLL)
    def _(step):
        firsts = [start + step * UNROLL for start in starts]
        for sub in range(UNROLL):
            for first, wide_ref, sum_ref in zip(firsts, wide_refs, sum_refs):
                picked = wide_ref[pl.ds(lookup_ref[first + sub], 1), :]
                sum_ref[pl.ds(lookup_ref[first + (sub + slots)], 1), :] += picked

    eye = diagonal()

    @pl.loop(0, rows // LANES)
    def _(block):
        at = pl.ds(pl.multiple_of(block * LANES, LANES), LANES)
        total = sum_refs[0][at, :]
        for sum_ref in sum_refs[1:]:
            total += sum_ref[at, :]
        if coded:
            codes, scale = encode(total + base_ref[at, :])
            out_ref[at, :] = codes
            scale_ref[block] = to_row(eye, scale)
        else:
            out_ref[at, :] = total


def scatter(places, slots, order, lookups, grads, rows, base=None):
    samples, feature = grads[0].shape
    smem = pl.BlockSpec(memory_space=pltpu.SMEM)
    vmem = pl.BlockSpec(memory_space=pltpu.VMEM)
    coded = base is not None
    total = jax.ShapeDtypeStruct((rows, feature), jnp.int16 if coded else jnp.float32)
    scales = jax.ShapeDtypeStruct((rows // LANES, 1, LANES), jnp.float32)
    more = [base] if coded else []
    return pl.pallas_call(
        functools.partial(scatter_kernel, places, slots, coded),
        out_shape=(total, scales) if coded else total,
        in_specs=[smem] * 2 + [vmem] * (len(grads) + len(more)),
        out_specs=(vmem, vmem) if coded else vmem,
        scratch_shapes=[pltpu.VMEM((samples, feature), jnp.float32)] * len(places)
        + [pltpu.VMEM((rows + 8, feature), jnp.float32)] * len(places),
        compiler_params=pltpu.CompilerParams(vmem_limit_bytes=40 << 20),
        cost_estimate=pl.CostEstimate(flops=0, bytes_accessed=COST_BYTES, transcendentals=0),
    )(order, lookups, *grads, *more)


def diagonal():
    shape = (LANES, LANES)
    return lax.broadcasted_iota(jnp.int32, shape, 0) == lax.broadcasted_iota(jnp.int32, shape, 1)


def to_row(eye, column):
    return jnp.sum(jnp.where(eye, column, 0.0), axis=0, keepdims=True)


def to_column(eye, row):
    return jnp.sum(jnp.where(eye, row, 0.0), axis=1, keepdims=True)


def encode(values):
    largest = jnp.max(jnp.abs(values), axis=1, keepdims=True)
    scale = jnp.maximum(largest, TINY) * (1.0 / CODE_MAX)
    return jnp.round(values * (1.0 / scale)).astype(jnp.int32).astype(jnp.int16), scale


def decode(codes, scale):
    return codes.astype(jnp.int32).astype(jnp.float32) * scale


def reduce_kernel(parts, code_ref, scale_ref, state_ref, out_ref, side_ref, *scratch):
    near_code, near_scale, sum_code, sum_scale, far_code, far_scale, send_sem, recv_sem = scratch
    copies, share, _ = code_ref.shape
    blocks = share // LANES
    pairs = copies // 2
    me = lax.axis_index("rep")
    pair, side = me // 2, lax.rem(me, 2)
    partner = pair * 2 + (1 - side)
    eye = diagonal()

    def other(step):
        return lax.rem(pair + step, pairs)

    def back(step):
        return lax.rem(pair + pairs - step, pairs)

    def send(phase, kind, step, part, source, target, device):
        copy = pltpu.make_async_remote_copy(
            src_ref=source,
            dst_ref=target,
            send_sem=send_sem.at[phase, kind, step, part],
            recv_sem=recv_sem.at[phase, kind, step, part],
            device_id={"rep": device},
            device_id_type=pl.DeviceIdType.MESH,
        )
        copy.start()
        return copy

    barrier = pltpu.get_barrier_semaphore()
    for peer in [partner] + [other(step) * 2 + side for step in range(1, pairs)]:
        pl.semaphore_signal(barrier, inc=1, device_id={"rep": peer}, device_id_type=pl.DeviceIdType.MESH)
    pl.semaphore_wait(barrier, pairs)

    steps = list(range(1, pairs)) + [0]
    part_blocks = blocks // parts
    near, far, hand, last = {}, {}, {}, {}

    def cut(ref, index, part):
        return ref.at[index, pl.ds(part * part_blocks, part_blocks)]

    def rows_of(ref, index, part):
        return ref.at[index, pl.ds(part * part_blocks * LANES, part_blocks * LANES)]

    def pair_sums(part):
        for step in steps[:-1]:
            for copy in near[step, part]:
                copy.wait_recv()
            chunk = other(step) * 2 + side

            @pl.loop(part * part_blocks, (part + 1) * part_blocks)
            def _(block):
                at = pl.ds(pl.multiple_of(block * LANES, LANES), LANES)
                total = decode(code_ref[chunk, at, :], to_column(eye, scale_ref[chunk, block]))
                total += decode(near_code[step, at, :], to_column(eye, near_scale[step, block]))
                codes, scale = encode(total)
                sum_code[step, at, :] = codes
                sum_scale[step, block] = to_row(eye, scale)

            far[step, part] = (
                send(1, 0, step, part, rows_of(sum_code, step, part), rows_of(far_code, step, part), chunk),
                send(1, 1, step, part, cut(sum_scale, step, part), cut(far_scale, step, part), chunk),
            )

    def share_out(phase, step, part, chunk, device):
        rows, rest = rows_of(out_ref, chunk, part), cut(side_ref, chunk, part)
        return send(phase, 0, step, part, rows, rows, device), send(phase, 1, step, part, rest, rest, device)

    def finish(part):
        for copy in near[0, part]:
            copy.wait_recv()
        for step in steps[:-1]:
            for copy in far[step, part]:
                copy.wait_recv()

        @pl.loop(part * part_blocks, (part + 1) * part_blocks)
        def _(block):
            at = pl.ds(pl.multiple_of(block * LANES, LANES), LANES)
            total = decode(code_ref[me, at, :], to_column(eye, scale_ref[me, block]))
            total += decode(near_code[0, at, :], to_column(eye, near_scale[0, block]))
            for step in steps[:-1]:
                total += decode(far_code[step, at, :], to_column(eye, far_scale[step, block]))
            codes, scale = encode(total)
            out_ref[me, at, :] = codes
            square = jnp.sum(total * total, axis=1, keepdims=True) * (1.0 / total.shape[1])
            updated = state_ref[me, block] + to_row(eye, square)
            side_ref[me, block, 0:1, :] = updated
            side_ref[me, block, 1:2, :] = to_row(eye, scale) / (jnp.sqrt(updated) + EPSILON)

        for step in range(1, pairs):
            hand[step, part] = share_out(2, step, part, me, other(step) * 2 + side)
        last[0, part] = share_out(3, 0, part, me, partner)

    def pass_on(part):
        for step in range(1, pairs):
            for copy in hand[step, part]:
                copy.wait_recv()
            last[step, part] = share_out(3, step, part, back(step) * 2 + side, partner)

    for part in range(parts):
        for step in steps:
            chunk = other(step) * 2 + (1 - side)
            near[step, part] = (
                send(0, 0, step, part, rows_of(code_ref, chunk, part), rows_of(near_code, step, part), partner),
                send(0, 1, step, part, cut(scale_ref, chunk, part), cut(near_scale, step, part), partner),
            )
    for turn in range(parts + 2):
        if turn < parts:
            pair_sums(turn)
        if 0 <= turn - 1 < parts:
            finish(turn - 1)
        if 0 <= turn - 2:
            pass_on(turn - 2)
    for key in last:
        for copy in last[key]:
            copy.wait_recv()
    for group in (near, far, hand, last):
        for sent in group.values():
            for copy in sent:
                copy.wait_send()


def reduce_rep(codes, scales, state):
    copies, share, feature = codes.shape
    blocks = share // LANES
    pairs = copies // 2
    vmem = pl.BlockSpec(memory_space=pltpu.VMEM)
    code_room = pltpu.VMEM((pairs, share, feature), jnp.int16)
    scale_room = pltpu.VMEM((pairs, blocks, 1, LANES), jnp.float32)
    parts = math.gcd(blocks, PARTS)
    semaphores = pltpu.SemaphoreType.DMA((4, 2, pairs, parts))
    return pl.pallas_call(
        functools.partial(reduce_kernel, parts),
        out_shape=(
            jax.ShapeDtypeStruct(codes.shape, jnp.int16),
            jax.ShapeDtypeStruct((copies, blocks, 2, LANES), jnp.float32),
        ),
        in_specs=[vmem] * 3,
        out_specs=(vmem, vmem),
        scratch_shapes=[code_room, scale_room] * 3
        + [semaphores, semaphores],
        compiler_params=pltpu.CompilerParams(
            collective_id=1, has_side_effects=True, vmem_limit_bytes=32 << 20
        ),
    )(codes, scales, state)


def shards(pooled_grad, slot_source, slot_target, slot_count, table_rows, accum):
    tables, feature = pooled_grad.shape[1:]
    rows_dev = table_rows.shape[1]
    rows = tables * rows_dev
    owner_total, slot_total = slot_source.shape[1:]
    copies = lax.axis_size("rep")
    me = lax.axis_index("rows")
    grads = pooled_grad.reshape(-1, feature)
    slot_ids = jnp.arange(slot_total, dtype=jnp.int32)
    filled = slot_ids[None, :] < slot_count[0][:, None]
    targets = jnp.where(filled, slot_target[0], rows)
    lookups = lax.all_to_all(
        jnp.stack([slot_source[0], targets], axis=1), "rows", split_axis=0, concat_axis=0, tiled=True
    )
    pieces = {0: grads}

    def swapped(places, span):
        swap = [(one, one ^ span) for one in range(owner_total)]
        pieces.update({place ^ span: lax.ppermute(pieces[place], "rows", swap) for place in places})

    half = owner_total // 2
    spans = [half >> shift for shift in range(1, half.bit_length())]
    swapped([0], half)
    for span in spans:
        swapped([place for place in list(pieces) if place < half], span)
    order = me ^ jnp.arange(owner_total, dtype=jnp.int32)
    halves = tuple(range(half)), tuple(range(half, owner_total))
    flat = lookups.reshape(-1)
    near = [pieces[place] for place in halves[0]]
    base = scatter(halves[0], slot_total, order, flat, near, rows)
    pieces[half], base = lax.optimization_barrier((pieces[half], base))
    for span in spans:
        swapped([place for place in list(pieces) if place >= half], span)
    far = [pieces[place] for place in halves[1]]
    codes, scales = scatter(halves[1], slot_total, order, flat, far, rows, base)
    share = rows // copies
    blocked = (copies, share // LANES, 1, LANES)
    all_codes, all_side = reduce_rep(
        codes.reshape(copies, share, feature), scales.reshape(blocked), accum.reshape(blocked)
    )
    new_accum = all_side[:, :, 0].reshape(tables, rows_dev)
    step = all_side[:, :, 1].reshape(tables, rows_dev, 1)
    move = all_codes.reshape(tables, rows_dev, feature).astype(jnp.float32) * step
    return table_rows - LEARN_RATE * move, new_accum


def solution(mesh):
    in_specs = (
        P(("rep", "rows"), None, None),
        P(("rep", "rows"), None, None),
        P(("rep", "rows"), None, None),
        P(("rep", "rows"), None),
        P(None, "rows", None),
        P(None, "rows"),
    )
    out_specs = (P(None, "rows", None), P(None, "rows"))
    return jax.shard_map(shards, mesh=mesh, in_specs=in_specs, out_specs=out_specs, check_vma=False)
```

```python
import functools
import math

import jax
import jax.numpy as jnp
from jax import lax
from jax.experimental import pallas as pl
from jax.experimental.pallas import tpu as pltpu
from jax.sharding import PartitionSpec as P

LEARN_RATE = 0.1
EPSILON = 1e-06
CODE_MAX = 32000.0
TINY = 1e-30
UNROLL = 16
BLOCK = 512
PARTS = 4
LANES = 128


def scatter_kernel(slots, count, order_ref, lookup_ref, *refs):
    grad_refs, (out_ref, scale_ref, *refs) = refs[:count], refs[count:]
    wide_refs, sum_refs = refs[:count], refs[count:]
    rows, feature = out_ref.shape
    for wide_ref, grad_ref in zip(wide_refs, grad_refs):
        wide_ref[...] = grad_ref[...].astype(jnp.float32)
    zeros = jnp.zeros((BLOCK, feature), jnp.float32)

    @pl.loop(0, rows // BLOCK)
    def _(block):
        for sum_ref in sum_refs:
            sum_ref[pl.ds(pl.multiple_of(block * BLOCK, BLOCK), BLOCK), :] = zeros

    starts = [order_ref[place] * (2 * slots) for place in range(count)]

    @pl.loop(0, slots // UNROLL)
    def _(step):
        firsts = [start + step * UNROLL for start in starts]
        for sub in range(UNROLL):
            for first, wide_ref, sum_ref in zip(firsts, wide_refs, sum_refs):
                picked = wide_ref[pl.ds(lookup_ref[first + sub], 1), :]
                sum_ref[pl.ds(lookup_ref[first + (sub + slots)], 1), :] += picked

    eye = diagonal()

    @pl.loop(0, rows // LANES)
    def _(block):
        at = pl.ds(pl.multiple_of(block * LANES, LANES), LANES)
        total = sum_refs[0][at, :]
        for sum_ref in sum_refs[1:]:
            total += sum_ref[at, :]
        codes, scale = encode(total)
        out_ref[at, :] = codes
        scale_ref[block] = to_row(eye, scale)


def scatter(order, lookups, grads, slots, rows):
    samples, feature = grads[0].shape
    count = len(grads)
    smem = pl.BlockSpec(memory_space=pltpu.SMEM)
    vmem = pl.BlockSpec(memory_space=pltpu.VMEM)
    return pl.pallas_call(
        functools.partial(scatter_kernel, slots, count),
        out_shape=(
            jax.ShapeDtypeStruct((rows, feature), jnp.int16),
            jax.ShapeDtypeStruct((rows // LANES, 1, LANES), jnp.float32),
        ),
        in_specs=[smem] * 2 + [vmem] * count,
        out_specs=(vmem, vmem),
        scratch_shapes=[pltpu.VMEM((samples, feature), jnp.float32)] * count
        + [pltpu.VMEM((rows + 8, feature), jnp.float32)] * count,
        compiler_params=pltpu.CompilerParams(vmem_limit_bytes=40 << 20),
    )(order, lookups, *grads)


def diagonal():
    shape = (LANES, LANES)
    return lax.broadcasted_iota(jnp.int32, shape, 0) == lax.broadcasted_iota(jnp.int32, shape, 1)


def to_row(eye, column):
    return jnp.sum(jnp.where(eye, column, 0.0), axis=0, keepdims=True)


def to_column(eye, row):
    return jnp.sum(jnp.where(eye, row, 0.0), axis=1, keepdims=True)


def encode(values):
    largest = jnp.max(jnp.abs(values), axis=1, keepdims=True)
    scale = jnp.maximum(largest, TINY) * (1.0 / CODE_MAX)
    return jnp.round(values * (1.0 / scale)).astype(jnp.int32).astype(jnp.int16), scale


def decode(codes, scale):
    return codes.astype(jnp.int32).astype(jnp.float32) * scale


def reduce_kernel(parts, code_ref, scale_ref, state_ref, out_ref, side_ref, *scratch):
    near_code, near_scale, sum_code, sum_scale, far_code, far_scale, send_sem, recv_sem = scratch
    copies, share, _ = code_ref.shape
    blocks = share // LANES
    pairs = copies // 2
    me = lax.axis_index("rep")
    pair, side = me // 2, lax.rem(me, 2)
    partner = pair * 2 + (1 - side)
    eye = diagonal()

    def other(step):
        return lax.rem(pair + step, pairs)

    def back(step):
        return lax.rem(pair + pairs - step, pairs)

    def send(phase, kind, step, part, source, target, device):
        copy = pltpu.make_async_remote_copy(
            src_ref=source,
            dst_ref=target,
            send_sem=send_sem.at[phase, kind, step, part],
            recv_sem=recv_sem.at[phase, kind, step, part],
            device_id={"rep": device},
            device_id_type=pl.DeviceIdType.MESH,
        )
        copy.start()
        return copy

    barrier = pltpu.get_barrier_semaphore()
    for peer in [partner] + [other(step) * 2 + side for step in range(1, pairs)]:
        pl.semaphore_signal(barrier, inc=1, device_id={"rep": peer}, device_id_type=pl.DeviceIdType.MESH)
    pl.semaphore_wait(barrier, pairs)

    steps = list(range(1, pairs)) + [0]
    part_blocks = blocks // parts
    near, far, hand, last = {}, {}, {}, {}

    def cut(ref, index, part):
        return ref.at[index, pl.ds(part * part_blocks, part_blocks)]

    def rows_of(ref, index, part):
        return ref.at[index, pl.ds(part * part_blocks * LANES, part_blocks * LANES)]

    def pair_sums(part):
        for step in steps[:-1]:
            for copy in near[step, part]:
                copy.wait_recv()
            chunk = other(step) * 2 + side

            @pl.loop(part * part_blocks, (part + 1) * part_blocks)
            def _(block):
                at = pl.ds(pl.multiple_of(block * LANES, LANES), LANES)
                total = decode(code_ref[chunk, at, :], to_column(eye, scale_ref[chunk, block]))
                total += decode(near_code[step, at, :], to_column(eye, near_scale[step, block]))
                codes, scale = encode(total)
                sum_code[step, at, :] = codes
                sum_scale[step, block] = to_row(eye, scale)

            far[step, part] = (
                send(1, 0, step, part, rows_of(sum_code, step, part), rows_of(far_code, step, part), chunk),
                send(1, 1, step, part, cut(sum_scale, step, part), cut(far_scale, step, part), chunk),
            )

    def share_out(phase, step, part, chunk, device):
        rows, rest = rows_of(out_ref, chunk, part), cut(side_ref, chunk, part)
        return send(phase, 0, step, part, rows, rows, device), send(phase, 1, step, part, rest, rest, device)

    def finish(part):
        for copy in near[0, part]:
            copy.wait_recv()
        for step in steps[:-1]:
            for copy in far[step, part]:
                copy.wait_recv()

        @pl.loop(part * part_blocks, (part + 1) * part_blocks)
        def _(block):
            at = pl.ds(pl.multiple_of(block * LANES, LANES), LANES)
            total = decode(code_ref[me, at, :], to_column(eye, scale_ref[me, block]))
            total += decode(near_code[0, at, :], to_column(eye, near_scale[0, block]))
            for step in steps[:-1]:
                total += decode(far_code[step, at, :], to_column(eye, far_scale[step, block]))
            codes, scale = encode(total)
            out_ref[me, at, :] = codes
            square = jnp.sum(total * total, axis=1, keepdims=True) * (1.0 / total.shape[1])
            updated = state_ref[me, block] + to_row(eye, square)
            side_ref[me, block, 0:1, :] = updated
            side_ref[me, block, 1:2, :] = to_row(eye, scale) / (jnp.sqrt(updated) + EPSILON)

        for step in range(1, pairs):
            hand[step, part] = share_out(2, step, part, me, other(step) * 2 + side)
        last[0, part] = share_out(3, 0, part, me, partner)

    def pass_on(part):
        for step in range(1, pairs):
            for copy in hand[step, part]:
                copy.wait_recv()
            last[step, part] = share_out(3, step, part, back(step) * 2 + side, partner)

    for part in range(parts):
        for step in steps:
            chunk = other(step) * 2 + (1 - side)
            near[step, part] = (
                send(0, 0, step, part, rows_of(code_ref, chunk, part), rows_of(near_code, step, part), partner),
                send(0, 1, step, part, cut(scale_ref, chunk, part), cut(near_scale, step, part), partner),
            )
    for turn in range(parts + 2):
        if turn < parts:
            pair_sums(turn)
        if 0 <= turn - 1 < parts:
            finish(turn - 1)
        if 0 <= turn - 2:
            pass_on(turn - 2)
    for key in last:
        for copy in last[key]:
            copy.wait_recv()
    for group in (near, far, hand, last):
        for sent in group.values():
            for copy in sent:
                copy.wait_send()


def reduce_rep(codes, scales, state):
    copies, share, feature = codes.shape
    blocks = share // LANES
    pairs = copies // 2
    vmem = pl.BlockSpec(memory_space=pltpu.VMEM)
    code_room = pltpu.VMEM((pairs, share, feature), jnp.int16)
    scale_room = pltpu.VMEM((pairs, blocks, 1, LANES), jnp.float32)
    parts = math.gcd(blocks, PARTS)
    semaphores = pltpu.SemaphoreType.DMA((4, 2, pairs, parts))
    return pl.pallas_call(
        functools.partial(reduce_kernel, parts),
        out_shape=(
            jax.ShapeDtypeStruct(codes.shape, jnp.int16),
            jax.ShapeDtypeStruct((copies, blocks, 2, LANES), jnp.float32),
        ),
        in_specs=[vmem] * 3,
        out_specs=(vmem, vmem),
        scratch_shapes=[code_room, scale_room] * 3
        + [semaphores, semaphores],
        compiler_params=pltpu.CompilerParams(
            collective_id=1, has_side_effects=True, vmem_limit_bytes=32 << 20
        ),
    )(codes, scales, state)


def shards(pooled_grad, slot_source, slot_target, slot_count, table_rows, accum):
    tables, feature = pooled_grad.shape[1:]
    rows_dev = table_rows.shape[1]
    rows = tables * rows_dev
    owner_total, slot_total = slot_source.shape[1:]
    copies = lax.axis_size("rep")
    me = lax.axis_index("rows")
    grads = pooled_grad.reshape(-1, feature)
    slot_ids = jnp.arange(slot_total, dtype=jnp.int32)
    filled = slot_ids[None, :] < slot_count[0][:, None]
    targets = jnp.where(filled, slot_target[0], rows)
    lookups = lax.all_to_all(
        jnp.stack([slot_source[0], targets], axis=1), "rows", split_axis=0, concat_axis=0, tiled=True
    )
    pieces = {0: grads}

    def swapped(places, span):
        swap = [(one, one ^ span) for one in range(owner_total)]
        pieces.update({place ^ span: lax.ppermute(pieces[place], "rows", swap) for place in places})

    span = owner_total // 2
    while span:
        swapped(list(pieces), span)
        span //= 2
    order = me ^ jnp.arange(owner_total, dtype=jnp.int32)
    codes, scales = scatter(
        order, lookups.reshape(-1), [pieces[place] for place in range(owner_total)], slot_total, rows
    )
    share = rows // copies
    blocked = (copies, share // LANES, 1, LANES)
    all_codes, all_side = reduce_rep(
        codes.reshape(copies, share, feature), scales.reshape(blocked), accum.reshape(blocked)
    )
    new_accum = all_side[:, :, 0].reshape(tables, rows_dev)
    step = all_side[:, :, 1].reshape(tables, rows_dev, 1)
    move = all_codes.reshape(tables, rows_dev, feature).astype(jnp.float32) * step
    return table_rows - LEARN_RATE * move, new_accum


def solution(mesh):
    in_specs = (
        P(("rep", "rows"), None, None),
        P(("rep", "rows"), None, None),
        P(("rep", "rows"), None, None),
        P(("rep", "rows"), None),
        P(None, "rows", None),
        P(None, "rows"),
    )
    out_specs = (P(None, "rows", None), P(None, "rows"))
    return jax.shard_map(shards, mesh=mesh, in_specs=in_specs, out_specs=out_specs, check_vma=False)
```

```python
import functools
import math

import jax
import jax.numpy as jnp
from jax import lax
from jax.experimental import pallas as pl
from jax.experimental.pallas import tpu as pltpu
from jax.sharding import PartitionSpec as P

LEARN_RATE = 0.1
EPSILON = 1e-06
CODE_MAX = 32000.0
TINY = 1e-30
UNROLL = 16
BLOCK = 512
PARTS = 4
LANES = 128


def scatter_kernel(slots, count, order_ref, lookup_ref, *refs):
    grad_refs, (out_ref, scale_ref, *refs) = refs[:count], refs[count:]
    wide_refs, sum_refs = refs[:count], refs[count:]
    rows, feature = out_ref.shape
    for wide_ref, grad_ref in zip(wide_refs, grad_refs):
        wide_ref[...] = grad_ref[...].astype(jnp.float32)
    zeros = jnp.zeros((BLOCK, feature), jnp.float32)

    @pl.loop(0, rows // BLOCK)
    def _(block):
        for sum_ref in sum_refs:
            sum_ref[pl.ds(pl.multiple_of(block * BLOCK, BLOCK), BLOCK), :] = zeros

    starts = [order_ref[place] * (2 * slots) for place in range(count)]

    @pl.loop(0, slots // UNROLL)
    def _(step):
        firsts = [start + step * UNROLL for start in starts]
        for sub in range(UNROLL):
            for first, wide_ref, sum_ref in zip(firsts, wide_refs, sum_refs):
                picked = wide_ref[pl.ds(lookup_ref[first + sub], 1), :]
                sum_ref[pl.ds(lookup_ref[first + (sub + slots)], 1), :] += picked

    eye = diagonal()

    @pl.loop(0, rows // LANES)
    def _(block):
        at = pl.ds(pl.multiple_of(block * LANES, LANES), LANES)
        total = sum_refs[0][at, :]
        for sum_ref in sum_refs[1:]:
            total += sum_ref[at, :]
        codes, scale = encode(total)
        out_ref[at, :] = codes
        scale_ref[block] = to_row(eye, scale)


def scatter(order, lookups, grads, slots, rows):
    samples, feature = grads[0].shape
    count = len(grads)
    smem = pl.BlockSpec(memory_space=pltpu.SMEM)
    vmem = pl.BlockSpec(memory_space=pltpu.VMEM)
    return pl.pallas_call(
        functools.partial(scatter_kernel, slots, count),
        out_shape=(
            jax.ShapeDtypeStruct((rows, feature), jnp.int16),
            jax.ShapeDtypeStruct((rows // LANES, 1, LANES), jnp.float32),
        ),
        in_specs=[smem] * 2 + [vmem] * count,
        out_specs=(vmem, vmem),
        scratch_shapes=[pltpu.VMEM((samples, feature), jnp.float32)] * count
        + [pltpu.VMEM((rows + 8, feature), jnp.float32)] * count,
        compiler_params=pltpu.CompilerParams(vmem_limit_bytes=40 << 20),
    )(order, lookups, *grads)


def diagonal():
    shape = (LANES, LANES)
    return lax.broadcasted_iota(jnp.int32, shape, 0) == lax.broadcasted_iota(jnp.int32, shape, 1)


def to_row(eye, column):
    return jnp.sum(jnp.where(eye, column, 0.0), axis=0, keepdims=True)


def to_column(eye, row):
    return jnp.sum(jnp.where(eye, row, 0.0), axis=1, keepdims=True)


def encode(values):
    largest = jnp.max(jnp.abs(values), axis=1, keepdims=True)
    scale = jnp.maximum(largest, TINY) * (1.0 / CODE_MAX)
    return jnp.round(values * (1.0 / scale)).astype(jnp.int32).astype(jnp.int16), scale


def decode(codes, scale):
    return codes.astype(jnp.int32).astype(jnp.float32) * scale


def reduce_kernel(parts, code_ref, scale_ref, state_ref, out_ref, side_ref, *scratch):
    near_code, near_scale, sum_code, sum_scale, far_code, far_scale, send_sem, recv_sem = scratch
    copies, share, _ = code_ref.shape
    blocks = share // LANES
    pairs = copies // 2
    me = lax.axis_index("rep")
    pair, side = me // 2, lax.rem(me, 2)
    partner = pair * 2 + (1 - side)
    eye = diagonal()

    def other(step):
        return lax.rem(pair + step, pairs)

    def back(step):
        return lax.rem(pair + pairs - step, pairs)

    def send(phase, kind, step, part, source, target, device):
        copy = pltpu.make_async_remote_copy(
            src_ref=source,
            dst_ref=target,
            send_sem=send_sem.at[phase, kind, step, part],
            recv_sem=recv_sem.at[phase, kind, step, part],
            device_id={"rep": device},
            device_id_type=pl.DeviceIdType.MESH,
        )
        copy.start()
        return copy

    barrier = pltpu.get_barrier_semaphore()
    for peer in [partner] + [other(step) * 2 + side for step in range(1, pairs)]:
        pl.semaphore_signal(barrier, inc=1, device_id={"rep": peer}, device_id_type=pl.DeviceIdType.MESH)
    pl.semaphore_wait(barrier, pairs)

    steps = list(range(1, pairs)) + [0]
    part_blocks = blocks // parts
    near, far, hand, last = {}, {}, {}, {}

    def cut(ref, index, part):
        return ref.at[index, pl.ds(part * part_blocks, part_blocks)]

    def rows_of(ref, index, part):
        return ref.at[index, pl.ds(part * part_blocks * LANES, part_blocks * LANES)]

    def pair_sums(part):
        for step in steps[:-1]:
            for copy in near[step, part]:
                copy.wait_recv()
            chunk = other(step) * 2 + side

            @pl.loop(part * part_blocks, (part + 1) * part_blocks)
            def _(block):
                at = pl.ds(pl.multiple_of(block * LANES, LANES), LANES)
                total = decode(code_ref[chunk, at, :], to_column(eye, scale_ref[chunk, block]))
                total += decode(near_code[step, at, :], to_column(eye, near_scale[step, block]))
                codes, scale = encode(total)
                sum_code[step, at, :] = codes
                sum_scale[step, block] = to_row(eye, scale)

            far[step, part] = (
                send(1, 0, step, part, rows_of(sum_code, step, part), rows_of(far_code, step, part), chunk),
                send(1, 1, step, part, cut(sum_scale, step, part), cut(far_scale, step, part), chunk),
            )

    def share_out(phase, step, part, chunk, device):
        rows, rest = rows_of(out_ref, chunk, part), cut(side_ref, chunk, part)
        return send(phase, 0, step, part, rows, rows, device), send(phase, 1, step, part, rest, rest, device)

    def finish(part):
        for copy in near[0, part]:
            copy.wait_recv()
        for step in steps[:-1]:
            for copy in far[step, part]:
                copy.wait_recv()

        @pl.loop(part * part_blocks, (part + 1) * part_blocks)
        def _(block):
            at = pl.ds(pl.multiple_of(block * LANES, LANES), LANES)
            total = decode(code_ref[me, at, :], to_column(eye, scale_ref[me, block]))
            total += decode(near_code[0, at, :], to_column(eye, near_scale[0, block]))
            for step in steps[:-1]:
                total += decode(far_code[step, at, :], to_column(eye, far_scale[step, block]))
            codes, scale = encode(total)
            out_ref[me, at, :] = codes
            square = jnp.sum(total * total, axis=1, keepdims=True) * (1.0 / total.shape[1])
            updated = state_ref[me, block] + to_row(eye, square)
            side_ref[me, block, 0:1, :] = updated
            side_ref[me, block, 1:2, :] = to_row(eye, scale) / (jnp.sqrt(updated) + EPSILON)

        for step in range(1, pairs):
            hand[step, part] = share_out(2, step, part, me, other(step) * 2 + side)
        last[0, part] = share_out(3, 0, part, me, partner)

    def pass_on(part):
        for step in range(1, pairs):
            for copy in hand[step, part]:
                copy.wait_recv()
            last[step, part] = share_out(3, step, part, back(step) * 2 + side, partner)

    for part in range(parts):
        for step in steps:
            chunk = other(step) * 2 + (1 - side)
            near[step, part] = (
                send(0, 0, step, part, rows_of(code_ref, chunk, part), rows_of(near_code, step, part), partner),
                send(0, 1, step, part, cut(scale_ref, chunk, part), cut(near_scale, step, part), partner),
            )
    for turn in range(parts + 2):
        if turn < parts:
            pair_sums(turn)
        if 0 <= turn - 1 < parts:
            finish(turn - 1)
        if 0 <= turn - 2:
            pass_on(turn - 2)
    for key in last:
        for copy in last[key]:
            copy.wait_recv()
    for group in (near, far, hand, last):
        for sent in group.values():
            for copy in sent:
                copy.wait_send()


def reduce_rep(codes, scales, state):
    copies, share, feature = codes.shape
    blocks = share // LANES
    pairs = copies // 2
    vmem = pl.BlockSpec(memory_space=pltpu.VMEM)
    code_room = pltpu.VMEM((pairs, share, feature), jnp.int16)
    scale_room = pltpu.VMEM((pairs, blocks, 1, LANES), jnp.float32)
    parts = math.gcd(blocks, PARTS)
    semaphores = pltpu.SemaphoreType.DMA((4, 2, pairs, parts))
    return pl.pallas_call(
        functools.partial(reduce_kernel, parts),
        out_shape=(
            jax.ShapeDtypeStruct(codes.shape, jnp.int16),
            jax.ShapeDtypeStruct((copies, blocks, 2, LANES), jnp.float32),
        ),
        in_specs=[vmem] * 3,
        out_specs=(vmem, vmem),
        scratch_shapes=[code_room, scale_room] * 3
        + [semaphores, semaphores],
        compiler_params=pltpu.CompilerParams(
            collective_id=1, has_side_effects=True, vmem_limit_bytes=32 << 20
        ),
    )(codes, scales, state)


def shards(pooled_grad, slot_source, slot_target, slot_count, table_rows, accum):
    tables, feature = pooled_grad.shape[1:]
    rows_dev = table_rows.shape[1]
    rows = tables * rows_dev
    owner_total, slot_total = slot_source.shape[1:]
    copies = lax.axis_size("rep")
    me = lax.axis_index("rows")
    grads = pooled_grad.reshape(-1, feature)
    slot_ids = jnp.arange(slot_total, dtype=jnp.int32)
    filled = slot_ids[None, :] < slot_count[0][:, None]
    targets = jnp.where(filled, slot_target[0], rows)
    lookups = lax.all_to_all(
        jnp.stack([slot_source[0], targets], axis=1), "rows", split_axis=0, concat_axis=0, tiled=True
    )
    pieces = {0: grads}

    def swapped(places, span):
        swap = [(one, one ^ span) for one in range(owner_total)]
        pieces.update({place ^ span: lax.ppermute(pieces[place], "rows", swap) for place in places})

    span = owner_total // 2
    while span:
        swapped(list(pieces), span)
        pieces[span], lookups = lax.optimization_barrier((pieces[span], lookups))
        span //= 2
    order = me ^ jnp.arange(owner_total, dtype=jnp.int32)
    codes, scales = scatter(
        order, lookups.reshape(-1), [pieces[place] for place in range(owner_total)], slot_total, rows
    )
    share = rows // copies
    blocked = (copies, share // LANES, 1, LANES)
    all_codes, all_side = reduce_rep(
        codes.reshape(copies, share, feature), scales.reshape(blocked), accum.reshape(blocked)
    )
    new_accum = all_side[:, :, 0].reshape(tables, rows_dev)
    step = all_side[:, :, 1].reshape(tables, rows_dev, 1)
    move = all_codes.reshape(tables, rows_dev, feature).astype(jnp.float32) * step
    return table_rows - LEARN_RATE * move, new_accum


def solution(mesh):
    in_specs = (
        P(("rep", "rows"), None, None),
        P(("rep", "rows"), None, None),
        P(("rep", "rows"), None, None),
        P(("rep", "rows"), None),
        P(None, "rows", None),
        P(None, "rows"),
    )
    out_specs = (P(None, "rows", None), P(None, "rows"))
    return jax.shard_map(shards, mesh=mesh, in_specs=in_specs, out_specs=out_specs, check_vma=False)
```
